32 devices in a mesh: grp: 2 (over core), dev: 16 (over z, y, x).
Axes of the slice: x: 2, y: 2, z: 4, core: 2. Of those that a mesh axis runs over, the one named last changes fastest.
Arguments:
- embeds_t: bfloat16 [1024, 131072], P(None, ('grp', 'dev'))
- shard_counts: int32 [32], P(('grp', 'dev')), may hold values from 512 to 4096, as said below
- assignments: int32 [64, 131072], P('dev', 'grp'), may hold values from 0 to 255
Outputs:
- whitened: bfloat16 [1024, 131072], P('dev', 'grp')
- factor: float32 [1024, 1024], replicated
- centroids: float32 [64, 16, 256], P('dev')
The draws below stay inside these ranges and needn't reach their ends.
Inputs may be any that keep to these rules, and one draw needn't show every extreme that they name: `shard_counts`: each shard holds between 512 and 4096 rows in its leading slots; one shard is full and one holds exactly 512.
All inputs are finite; a program needn't handle non-finite values.
Results may differ from the reference program's by a relative error of at most 0.0029.
Values may be sent and summed in bfloat16 or wider, within the bound.
A program may use at most 192 MiB of HBM per device.

```python
import math
import jax
import jax.numpy as jnp
from jax import lax

D = 1024
SUBS = 64
CENT = 256
ROW_DEV = 4096
SUBW = 16
SHARDS = 32
ROWS = 131072


def draw_embeds_t(key, part):
    key_scale = jax.random.fold_in(key, 11)
    key_offset = jax.random.fold_in(key, 12)
    key_rows = jax.random.fold_in(key, 13)
    key_noise = jax.random.fold_in(key, 14)
    col_scale = jnp.exp(jax.random.uniform(key_scale, (D, 1), jnp.float32) * math.log(10.0))
    offset = jax.random.uniform(key_offset, (D, 1), jnp.float32, -10.0, 10.0) * col_scale
    row_scale = jnp.exp(jax.random.uniform(key_rows, (1, ROWS), jnp.float32) * math.log(3.0))
    noise_part = jax.random.normal(key_noise, (D, ROWS), jnp.float32)
    values = offset + col_scale * row_scale * noise_part
    return values.astype(jnp.bfloat16)


def draw_shard_counts(key, part):
    key_first = jax.random.fold_in(key, 21)
    key_second = jax.random.fold_in(key, 22)
    key_order = jax.random.fold_in(key, 23)
    low_count = ROW_DEV // 8
    count_span = ROW_DEV - low_count
    first_draw = jax.random.randint(key_first, (SHARDS,), 0, count_span + 1)
    second_draw = jax.random.randint(key_second, (SHARDS,), 0, count_span + 1)
    raw_counts = low_count + first_draw * second_draw // max(count_span, 1)
    order_ids = jax.random.permutation(key_order, SHARDS)
    raw_counts = jnp.where(order_ids == 0, ROW_DEV, jnp.where(order_ids == 1, low_count, raw_counts))
    return raw_counts.astype(jnp.int32)


def place_ends(values, rng, low, high):
    dims = values.shape
    spot = [jax.random.randint(jax.random.fold_in(rng, axis), (), 0, dims[axis]) for axis in range(len(dims))]
    values = values.at[tuple(spot)].set(low)
    longest = dims.index(max(dims))
    spot[longest] = (spot[longest] + 1) % dims[longest]
    return values.at[tuple(spot)].set(high)


def setup_inputs(seed: int = 0) -> dict:
    keys = jax.random.split(jax.random.key(seed), 4)
    embeds_t = draw_embeds_t(jax.random.fold_in(keys[3], 71), 0)
    shard_counts = draw_shard_counts(jax.random.fold_in(keys[3], 71), 0)
    assignments = place_ends(jax.random.randint(keys[2], (SUBS, ROWS), 0, CENT), jax.random.fold_in(keys[2], 1), 0, CENT - 1).astype(jnp.int32)
    return dict(embeds_t=embeds_t, shard_counts=shard_counts, assignments=assignments)


def reference(embeds_t, shard_counts, assignments):
    slot_ids = jnp.arange(ROW_DEV, dtype=jnp.int32)
    valid_sh = (slot_ids[None, :] < shard_counts[:, None]).astype(jnp.float32)
    total_rows = jnp.sum(shard_counts).astype(jnp.float32)
    blocks = embeds_t.reshape(D, SHARDS, ROW_DEV).transpose(1, 0, 2)

    def add_cols(carry, items):
        blk_data, blk_valid = items
        return (carry + jnp.sum(blk_data.astype(jnp.float32) * blk_valid[None, :], axis=1), None)
    col_sum, _ = lax.scan(add_cols, jnp.zeros((D,), jnp.float32), (blocks, valid_sh))
    col_mean = col_sum / total_rows

    def centre(blk_data, blk_valid):
        return (blk_data.astype(jnp.float32) - col_mean[:, None]) * blk_valid[None, :]

    def add_gram(carry, items):
        centred = centre(items[0], items[1])
        return (carry + jnp.dot(centred.astype(jnp.float32), centred.T.astype(jnp.float32), precision=lax.Precision.HIGHEST, preferred_element_type=jnp.float32), None)
    gram_sum, _ = lax.scan(add_gram, jnp.zeros((D, D), jnp.float32), (blocks, valid_sh))
    factor = jnp.linalg.cholesky(gram_sum / (total_rows - 1.0))

    def whiten(items):
        centred = centre(items[0], items[1])
        return lax.linalg.triangular_solve(factor, centred, left_side=True, lower=True).astype(jnp.bfloat16)
    white_blocks = lax.map(whiten, (blocks, valid_sh))
    whitened = white_blocks.transpose(1, 0, 2).reshape(D, SHARDS * ROW_DEV)
    valid_rows = valid_sh.reshape(-1)

    def per_sub(sub_index):
        sub_rows = lax.dynamic_slice_in_dim(whitened, sub_index * SUBW, SUBW, 0).astype(jnp.float32)
        sub_assign = lax.dynamic_index_in_dim(assignments, sub_index, 0, keepdims=False)
        cent_sums = jax.ops.segment_sum(sub_rows.T * valid_rows[:, None], sub_assign, CENT)
        cent_counts = jax.ops.segment_sum(valid_rows, sub_assign, CENT)
        return cent_sums.T / (cent_counts[None, :] + 1.0)
    centroids = lax.map(per_sub, jnp.arange(SUBS, dtype=jnp.int32))
    return (whitened, factor, centroids)
```

```python
import functools

import jax
import jax.numpy as jnp
from jax import lax
from jax.experimental import pallas as pl
from jax.experimental.pallas import tpu as pltpu
from jax.sharding import PartitionSpec as P

CENT = 256
BAND = 256
BLK = 128
PANEL = 8
HIGH = lax.Precision.HIGHEST
NT = (((1,), (1,)), ((), ()))
NN = (((1,), (0,)), ((), ()))


def params():
    return pltpu.CompilerParams(
        dimension_semantics=("arbitrary",), vmem_limit_bytes=60000 * 1024
    )


def gram_kernel(cnt, x_ref, gram_ref, shift_ref, sum_ref, hi_ref, lo_ref):
    step = pl.program_id(0)
    d, blk = x_ref.shape
    bands = d // BAND

    @pl.when(step == 0)
    def _():
        gram_ref[...] = jnp.zeros_like(gram_ref)
        sum_ref[...] = jnp.zeros_like(sum_ref)
        for r in range(bands):
            rows = pl.ds(r * BAND, BAND)
            mean = jnp.sum(x_ref[rows, :].astype(jnp.float32), axis=1, keepdims=True) * (1.0 / blk)
            shift_ref[rows, :] = mean.astype(jnp.bfloat16).astype(jnp.float32)

    @pl.when(step * blk < cnt[0])
    def _():
        ok = (step * blk + lax.broadcasted_iota(jnp.int32, (1, blk), 1)) < cnt[0]
        for r in range(bands):
            rows = pl.ds(r * BAND, BAND)
            y = jnp.where(ok, x_ref[rows, :].astype(jnp.float32) - shift_ref[rows, :], 0.0)
            sum_ref[rows, :] += jnp.sum(y, axis=1, keepdims=True)
            hi = y.astype(jnp.bfloat16)
            hi_ref[rows, :] = hi
            lo_ref[rows, :] = (y - hi.astype(jnp.float32)).astype(jnp.bfloat16)
        out = 0
        for r in range(bands):
            hr = hi_ref[pl.ds(r * BAND, BAND), :]
            lr = lo_ref[pl.ds(r * BAND, BAND), :]
            for c in range(r + 1):
                hc = hi_ref[pl.ds(c * BAND, BAND), :]
                lc = lo_ref[pl.ds(c * BAND, BAND), :]
                dot = functools.partial(
                    lax.dot_general, dimension_numbers=NT, preferred_element_type=jnp.float32
                )
                gram_ref[pl.ds(out * BAND, BAND), :] += dot(hr, hc) + dot(hr, lc) + dot(lr, hc)
                out += 1


def gram_call(counts, x):
    d, n = x.shape
    blk = min(512, n)
    bands = d // BAND
    tiles = bands * (bands + 1) // 2
    return pl.pallas_call(
        gram_kernel,
        grid_spec=pltpu.PrefetchScalarGridSpec(
            num_scalar_prefetch=1,
            grid=(n // blk,),
            in_specs=[pl.BlockSpec((d, blk), lambda i, c: (0, i))],
            out_specs=[
                pl.BlockSpec((tiles * BAND, BAND), lambda i, c: (0, 0)),
                pl.BlockSpec((d, 1), lambda i, c: (0, 0)),
                pl.BlockSpec((d, 1), lambda i, c: (0, 0)),
            ],
            scratch_shapes=[pltpu.VMEM((d, blk), jnp.bfloat16)] * 2,
        ),
        out_shape=[
            jax.ShapeDtypeStruct((tiles * BAND, BAND), jnp.float32),
            jax.ShapeDtypeStruct((d, 1), jnp.float32),
            jax.ShapeDtypeStruct((d, 1), jnp.float32),
        ],
        compiler_params=params(),
    )(counts, x)


def factor_block(s_ref, m_ref, u_ref):
    rows = lax.broadcasted_iota(jnp.int32, (BLK, 1), 0)
    lanes = lax.broadcasted_iota(jnp.int32, (1, BLK), 1)
    sub = lax.broadcasted_iota(jnp.int32, (PANEL, 1), 0)
    m_ref[...] = (rows == lanes).astype(jnp.float32)

    def panel(step, carry):
        j = pl.multiple_of(step * PANEL, PANEL)
        s = s_ref[...]
        top = s_ref[pl.ds(j, PANEL), :]
        inv_top = m_ref[pl.ds(j, PANEL), :]
        cols = [
            jnp.sum(jnp.where(lanes == j + b, s, 0.0), axis=1, keepdims=True) for b in range(PANEL)
        ]
        small = [
            jnp.sum(jnp.where(lanes == j + b, top, 0.0), axis=1, keepdims=True)
            for b in range(PANEL)
        ]
        for b in range(PANEL):
            p = small[b][b : b + 1, :]
            inv = lax.rsqrt(p)
            inv = inv * (1.5 - 0.5 * p * inv * inv)
            head = small[b] * inv
            col = cols[b] * inv
            cols[b] = col
            below = jnp.where(sub > b, head, 0.0)
            row = top[b : b + 1, :] * inv
            inv_row = inv_top[b : b + 1, :] * inv
            top = jnp.where(sub == b, row, top - below * row)
            inv_top = jnp.where(sub == b, inv_row, inv_top - below * inv_row)
            for c in range(b + 1, PANEL):
                f = head[c : c + 1, :]
                small[c] = small[c] - head * f
                cols[c] = cols[c] - col * f
        u_ref[pl.ds(j, PANEL), :] = top
        m = m_ref[...]
        for b in range(PANEL):
            col = jnp.where(rows >= j + PANEL, cols[b], 0.0)
            s = s - col * top[b : b + 1, :]
            m = m - col * inv_top[b : b + 1, :]
        s_ref[...] = s
        m_ref[...] = m
        m_ref[pl.ds(j, PANEL), :] = inv_top
        return carry

    lax.fori_loop(0, BLK // PANEL, panel, 0)


def factor_kernel(
    gram_ref, left_ref, right_ref, scale_ref, mean_ref, l_ref, whi_ref, wlo_ref, c_ref,
    a_ref, w_ref, s_ref, m_ref, u_ref,
):
    d = l_ref.shape[0]
    n = d // BLK
    dot = functools.partial(lax.dot_general, precision=HIGH, preferred_element_type=jnp.float32)
    l_ref[...] = jnp.zeros_like(l_ref)
    w_ref[...] = jnp.zeros_like(w_ref)
    scale = scale_ref[0, 0]
    out = 0
    for r in range(d // BAND):
        for c in range(r + 1):
            fix = dot(
                left_ref[pl.ds(r * BAND, BAND), :], right_ref[pl.ds(c * BAND, BAND), :],
                dimension_numbers=NT,
            )
            a_ref[pl.ds(r * BAND, BAND), pl.ds(c * BAND, BAND)] = (
                gram_ref[pl.ds(out * BAND, BAND), :] + fix
            ) * scale
            out += 1
    for k in range(n):
        lo, hi = k * BLK, (k + 1) * BLK
        s_ref[...] = a_ref[lo:hi, lo:hi]
        factor_block(s_ref, m_ref, u_ref)
        rows = lax.broadcasted_iota(jnp.int32, (BLK, BLK), 0)
        lanes = lax.broadcasted_iota(jnp.int32, (BLK, BLK), 1)
        l_ref[lo:hi, lo:hi] = jnp.where(rows >= lanes, u_ref[...].T, 0.0)
        inv = jnp.where(rows >= lanes, m_ref[...], 0.0)
        w_ref[lo:hi, lo:hi] = inv
        if k:
            part = dot(l_ref[lo:hi, :lo], w_ref[:lo, :lo], dimension_numbers=NN)
            w_ref[lo:hi, :lo] = -dot(inv, part, dimension_numbers=NN)
        if hi < d:
            l_ref[hi:, lo:hi] = dot(a_ref[hi:, lo:hi], inv, dimension_numbers=NT)
            for i in range(hi, d, BLK):
                a_ref[i:, i : i + BLK] -= dot(
                    l_ref[i:, lo:hi], l_ref[i : i + BLK, lo:hi], dimension_numbers=NT
                )
    for k in range(n):
        rows = pl.ds(k * BLK, BLK)
        w = w_ref[rows, :]
        w_hi = w.astype(jnp.bfloat16)
        w_lo = (w - w_hi.astype(jnp.float32)).astype(jnp.bfloat16)
        whi_ref[rows, :] = w_hi
        wlo_ref[rows, :] = w_lo
        both = w_hi.astype(jnp.float32) + w_lo.astype(jnp.float32)
        c_ref[rows, :] = jnp.sum(both * mean_ref[...], axis=1, keepdims=True)


def factor_call(gram, left, right, scale, mean):
    d = left.shape[0]
    vm = pl.BlockSpec(memory_space=pltpu.VMEM)
    return pl.pallas_call(
        factor_kernel,
        in_specs=[vm, vm, vm, pl.BlockSpec(memory_space=pltpu.SMEM), vm],
        out_specs=[vm] * 4,
        out_shape=[
            jax.ShapeDtypeStruct((d, d), jnp.float32),
            jax.ShapeDtypeStruct((d, d), jnp.bfloat16),
            jax.ShapeDtypeStruct((d, d), jnp.bfloat16),
            jax.ShapeDtypeStruct((d, 1), jnp.float32),
        ],
        scratch_shapes=[pltpu.VMEM((d, d), jnp.float32)] * 2
        + [pltpu.VMEM((BLK, BLK), jnp.float32)] * 3,
        compiler_params=pltpu.CompilerParams(vmem_limit_bytes=60000 * 1024),
    )(gram, left, right, scale, mean)


def whiten_kernel(cnt, x_ref, whi_ref, wlo_ref, c_ref, out_ref):
    step = pl.program_id(0)
    d, blk = x_ref.shape
    live = step * blk < cnt[0]

    @pl.when(live)
    def _():
        ok = (step * blk + lax.broadcasted_iota(jnp.int32, (1, blk), 1)) < cnt[0]
        for r in range(d // BAND):
            rows = pl.ds(r * BAND, BAND)
            k = (r + 1) * BAND
            x = x_ref[:k, :]
            y = jnp.dot(whi_ref[rows, :k], x, preferred_element_type=jnp.float32)
            y += jnp.dot(wlo_ref[rows, :k], x, preferred_element_type=jnp.float32)
            out_ref[rows, :] = jnp.where(ok, y - c_ref[rows, :], 0.0).astype(jnp.bfloat16)

    @pl.when(jnp.logical_not(live))
    def _():
        out_ref[...] = jnp.zeros_like(out_ref)


def whiten_call(counts, x, w_hi, w_lo, c):
    d, n = x.shape
    blk = min(512, n)
    whole = lambda i, c: (0, 0)
    return pl.pallas_call(
        whiten_kernel,
        grid_spec=pltpu.PrefetchScalarGridSpec(
            num_scalar_prefetch=1,
            grid=(n // blk,),
            in_specs=[
                pl.BlockSpec((d, blk), lambda i, c: (0, i)),
                pl.BlockSpec((d, d), whole),
                pl.BlockSpec((d, d), whole),
                pl.BlockSpec((d, 1), whole),
            ],
            out_specs=pl.BlockSpec((d, blk), lambda i, c: (0, i)),
        ),
        out_shape=jax.ShapeDtypeStruct((d, n), jnp.bfloat16),
        compiler_params=params(),
    )(counts, x, w_hi, w_lo, c)


HI = 4
LO = CENT // HI


def seg_kernel(sub_width, row_dev, cnt, x_ref, a_ref, out_ref):
    step = pl.program_id(0)
    subs, blk = a_ref.shape
    per = row_dev // blk
    limit = cnt[step // per] - (step % per) * blk

    @pl.when(step == 0)
    def _():
        out_ref[...] = jnp.zeros_like(out_ref)

    @pl.when(limit > 0)
    def _():
        ok = lax.broadcasted_iota(jnp.int32, (1, blk), 1) < limit
        cent = lax.broadcasted_iota(jnp.int32, (LO, blk), 0)
        pad = lax.broadcasted_iota(jnp.int32, (sub_width, blk), 0)
        for s in range(subs):
            ids = jnp.where(ok, a_ref[s : s + 1, :], -1)
            high, low = ids // LO, ids % LO
            high = jnp.where(ok, high, -1)
            low_hot = (cent == low).astype(jnp.float32).astype(jnp.bfloat16)
            x = x_ref[s * sub_width : (s + 1) * sub_width, :].astype(jnp.float32)
            parts = [jnp.where(high == h, x, 0.0).astype(jnp.bfloat16) for h in range(HI)]
            parts.append((pad == high).astype(jnp.float32).astype(jnp.bfloat16))
            out_ref[s] += lax.dot_general(
                jnp.concatenate(parts, axis=0), low_hot, NT, preferred_element_type=jnp.float32
            )


def seg_call(limits, owned, assign, row_dev):
    subs, n = assign.shape
    width = owned.shape[0] // subs
    blk = min(1024, row_dev)
    rows = (HI + 1) * width
    return pl.pallas_call(
        functools.partial(seg_kernel, width, row_dev),
        grid_spec=pltpu.PrefetchScalarGridSpec(
            num_scalar_prefetch=1,
            grid=(n // blk,),
            in_specs=[
                pl.BlockSpec((subs * width, blk), lambda i, c: (0, i)),
                pl.BlockSpec((subs, blk), lambda i, c: (0, i)),
            ],
            out_specs=pl.BlockSpec((subs, rows, LO), lambda i, c: (0, 0, 0)),
        ),
        out_shape=jax.ShapeDtypeStruct((subs, rows, LO), jnp.float32),
        compiler_params=params(),
    )(limits, owned, assign)


def body(embeds_t, shard_counts, assignments):
    both = ("grp", "dev")
    row_dev = embeds_t.shape[1]
    counts_all = lax.all_gather(shard_counts, both, axis=0, tiled=True)
    gram_part, shift, col_sum = gram_call(shard_counts, embeds_t)
    stats = lax.all_gather(jnp.concatenate([shift, col_sum], axis=1).T, both, axis=0)
    gram = lax.psum(gram_part, both)
    n = counts_all.astype(jnp.float32)[:, None]
    total = jnp.sum(counts_all).astype(jnp.float32)
    shifts, sums = stats[:, 0, :], stats[:, 1, :]
    mean = jnp.sum(sums + n * shifts, axis=0, keepdims=True) / total
    off = shifts + sums / n - mean
    left = jnp.concatenate([-sums / n, off * n], axis=0).T
    right = jnp.concatenate([sums, off], axis=0).T
    scale = (1.0 / (total - 1.0)).reshape(1, 1)
    factor, w_hi, w_lo, c = factor_call(gram, left, right, scale, mean)
    white = whiten_call(shard_counts, embeds_t, w_hi, w_lo, c)
    owned = lax.all_to_all(white, "dev", split_axis=0, concat_axis=1, tiled=True)
    subs = assignments.shape[0]
    width = owned.shape[0] // subs
    num_dev = lax.axis_size("dev")
    limits = lax.dynamic_slice_in_dim(counts_all, lax.axis_index("grp") * num_dev, num_dev)
    acc = lax.psum(seg_call(limits, owned, assignments, row_dev), "grp")
    acc = acc.reshape(subs, HI + 1, width, LO).transpose(0, 2, 1, 3)
    cent_sums = acc[:, :, :HI].reshape(subs, width, CENT)
    cent_counts = acc[:, :HI, HI].reshape(subs, 1, CENT)
    return owned, factor, cent_sums / (cent_counts + 1.0)


def solution(mesh):
    return jax.shard_map(
        body,
        mesh=mesh,
        in_specs=(P(None, ("grp", "dev")), P(("grp", "dev")), P("dev", "grp")),
        out_specs=(P("dev", "grp"), P(), P("dev", None, None)),
        check_vma=False,
    )
```
